32 devices in a mesh: section: 4 (over y, x), row: 4 (over z), col: 2 (over core).
Axes of the slice: x: 2, y: 2, z: 4, core: 2. Of those that a mesh axis runs over, the one named last changes fastest.
Arguments:
- stash: bfloat16 [4, 2, 1024, 6144], P('section', None, 'col', 'row'), may hold values from -6 to 6
- slot: int32 [4], P('section'), may hold values from 0 to 1
- cotangent: bfloat16 [4, 1024, 6144], P('section', 'col', 'row'), may hold values from -6 to 6
- w_first: bfloat16 [4, 6144, 14336], P('section', 'row', 'col'), may hold values from -0.109375 to 0.109375
- mask_first: int32 [4, 48, 112], P('section', 'row', 'col'), may hold values 0 or 1
- w_second: bfloat16 [4, 14336, 6144], P('section', 'col', 'row'), may hold values from -0.0625 to 0.0625
- mask_second: int32 [4, 112, 48], P('section', 'col', 'row'), may hold values 0 or 1
Outputs:
- grad_previous: bfloat16 [4, 1024, 6144], P('section', 'col', 'row')
- grad_first: bfloat16 [4, 6144, 14336], P('section', 'row', 'col')
- grad_second: bfloat16 [4, 14336, 6144], P('section', 'col', 'row')
The draws below stay inside these ranges and needn't reach their ends.
Inputs may be any that keep to these rules, and one draw needn't show every extreme that they name: `mask_first`: each entry is 0 (block absent) or 1 (block present). `mask_second`: each entry is 0 (block absent) or 1 (block present).
All inputs are finite; a program needn't handle non-finite values.
Results may differ from the reference program's by a relative error of at most 0.015.
Values may be sent and summed in bfloat16 or wider, within the bound.
A program may use at most 320 MiB of HBM per device.

```python
import jax
import jax.numpy as jnp
from jax import lax

D = 6144
FF = 14336
BLK = 128
MB = 1024
STASH = 2
DBLK = 48
FBLK = 112
N_SECTION = 4
N_ROW = 4
N_COL = 2


def plant(entries, rng, smallest, top_value):
    shape = entries.shape
    index_at = [jax.random.randint(jax.random.fold_in(rng, axis), (), 0, shape[axis]) for axis in range(len(shape))]
    entries = entries.at[tuple(index_at)].set(smallest)
    longest = shape.index(max(shape))
    index_at[longest] = (index_at[longest] + 1) % shape[longest]
    return entries.at[tuple(index_at)].set(top_value)


def levels(rng, dims, shards, low, top_value):
    factor_of = 1.0
    for dim, blocks in shards:
        steps = jax.random.uniform(jax.random.fold_in(jax.random.fold_in(rng, 6), dim), (blocks,), jnp.float32, low / len(shards), top_value / len(shards))
        factor_of = factor_of * jnp.repeat(jnp.exp(steps), dims[dim] // blocks).reshape((-1,) + (1,) * (len(dims) - 1 - dim))
    return factor_of


def noise(stream_key, shape, scale, most, split=(), kind=jnp.bfloat16):
    entries = scale * jax.random.normal(stream_key, shape, jnp.float32)
    if split:
        entries = entries * levels(stream_key, shape, split, -0.22, 0.18)
    return jnp.clip(entries, -most, most).astype(kind)


def setup_inputs(seed: int = 0) -> dict:
    keys = jax.random.split(jax.random.key(seed), 8)
    stash = noise(keys[0], (N_SECTION, STASH, MB, D), 1.0, 6.0, ((0, 4), (2, 2), (3, 4)))
    slot = plant(jax.random.randint(keys[1], (N_SECTION,), 0, STASH), jax.random.fold_in(keys[1], 1), 0, STASH - 1).astype(jnp.int32)
    cotangent = noise(keys[2], (N_SECTION, MB, D), 1.0, 6.0, ((0, 4), (1, 2), (2, 4)))
    w_first = noise(keys[3], (N_SECTION, D, FF), (D // 2) ** -0.5, 0.109375, ((0, 4), (1, 4), (2, 2)))
    mask_first = plant((jax.random.randint(keys[4], (N_SECTION, DBLK, FBLK), 0, 2) < 1).astype(jnp.int32), jax.random.fold_in(keys[4], 1), 0, 1)
    w_second = noise(keys[5], (N_SECTION, FF, D), (FF // 2) ** -0.5, 0.0625, ((0, 4), (1, 2), (2, 4)))
    mask_second = plant((jax.random.randint(keys[6], (N_SECTION, FBLK, DBLK), 0, 2) < 1).astype(jnp.int32), jax.random.fold_in(keys[6], 1), 0, 1)
    return {"stash": stash, "slot": slot, "cotangent": cotangent, "w_first": w_first, "mask_first": mask_first, "w_second": w_second, "mask_second": mask_second}


def apply_blocks(weight, blocks_on):
    height, breadth = weight.shape
    shaped = weight.reshape(height // BLK, BLK, breadth // BLK, BLK)
    shaped = shaped * blocks_on.astype(weight.dtype)[:, None, :, None]
    return shaped.reshape(height, breadth)


def banded(left, right, bands):
    width = left.shape[1] // bands
    total = jnp.zeros((left.shape[0], right.shape[1]), jnp.float32)
    for index in range(bands):
        part = jnp.dot(left[:, index * width:(index + 1) * width], right[index * width:(index + 1) * width, :], preferred_element_type=jnp.float32)
        total = total + part.astype(jnp.bfloat16).astype(jnp.float32)
    return total


def one_section(packed):
    saved, choose, upstream, first_raw, first_mask, second_raw, second_mask = packed
    inputs = lax.dynamic_index_in_dim(saved, choose.astype(jnp.int32), 0, keepdims=False)
    sparse_first = apply_blocks(first_raw, first_mask)
    sparse_second = apply_blocks(second_raw, second_mask)
    preact = banded(inputs, sparse_first, N_ROW)
    back = banded(upstream, sparse_second.T, N_ROW)
    sigmoid_val = jax.nn.sigmoid(preact)
    hidden = (preact * sigmoid_val).astype(jnp.bfloat16)
    hidden_grad = (back * sigmoid_val * (1.0 + preact * (1.0 - sigmoid_val))).astype(jnp.bfloat16)
    grad_first = apply_blocks(jnp.dot(inputs.T, hidden_grad, preferred_element_type=jnp.float32), first_mask).astype(jnp.bfloat16)
    grad_second = apply_blocks(jnp.dot(hidden.T, upstream, preferred_element_type=jnp.float32), second_mask).astype(jnp.bfloat16)
    input_grad = (upstream.astype(jnp.float32) + banded(hidden_grad, sparse_first.T, N_COL)).astype(jnp.bfloat16)
    return input_grad, grad_first, grad_second


def reference(stash, slot, cotangent, w_first, mask_first, w_second, mask_second):
    input_grad, grad_first, grad_second = lax.map(one_section, (stash, slot, cotangent, w_first, mask_first, w_second, mask_second))
    grad_previous = jnp.roll(input_grad, -1, axis=0)
    return grad_previous, grad_first, grad_second
```

```python
import functools

import jax
import jax.numpy as jnp
from jax import lax
from jax.experimental import pallas as pl
from jax.experimental.pallas import tpu as pltpu
from jax.sharding import PartitionSpec as P

BLK = 128
MOST_CHUNKS = 14
WIDTH = 256
PIECES = 2
MESH = pl.DeviceIdType.MESH


def contract(left, right, left_dim, right_dim):
    return lax.dot_general(
        left, right, (((left_dim,), (right_dim,)), ((), ())), preferred_element_type=jnp.float32
    )


def wide(value):
    return value.astype(jnp.float32)


def tick_kernel(
    n_row, ring, pieces,
    x_hbm, up_hbm, w1_hbm, w2_hbm, m1_ref, m2_ref,
    ig_hbm, g1_hbm, g2_hbm,
    x_v, up_v, acc, w1_buf, w2_buf, w1_m, w2_m, part, came, send, hid, hgr, g1_buf, g2_buf, swap_out, swap_in,
    load_sem, swap_send, swap_recv, w_sem, send_sem, recv_sem, g_sem, credit,
):
    me, core = lax.axis_index("row"), lax.axis_index("col")
    other = 1 - core
    tokens, depth = x_v.shape
    half = tokens // 2
    chunks, width = m1_ref.shape[0], w1_buf.shape[2]
    last = n_row - 1
    tile = min(256, half)
    tiles = tokens // tile

    def rows(i, size=tile):
        return pl.ds(pl.multiple_of(i * size, size), size)

    barrier = pltpu.get_barrier_semaphore()
    pl.semaphore_signal(barrier, inc=1, device_id={"col": other}, device_id_type=MESH)

    @pl.when(me > 0)
    def _():
        pl.semaphore_signal(barrier, inc=1, device_id={"row": me - 1}, device_id_type=MESH)

    @pl.when(me < last)
    def _():
        pl.semaphore_signal(barrier, inc=1, device_id={"row": me + 1}, device_id_type=MESH)

    def weights(t, which):
        k = lax.rem(t, 2)
        at = pl.ds(pl.multiple_of(t * width, width), width)
        if which == 0:
            return pltpu.make_async_copy(w2_hbm.at[at], w2_buf.at[k], w_sem.at[0, k])
        return pltpu.make_async_copy(w1_hbm.at[:, at], w1_buf.at[k], w_sem.at[1, k])

    mine, theirs = rows(core, half), rows(other, half)
    own_up = pltpu.make_async_copy(up_hbm, up_v.at[mine], load_sem.at[0])
    own_x = pltpu.make_async_copy(x_hbm, x_v.at[mine], load_sem.at[1])
    own_up.start()
    weights(0, 0).start()
    own_x.start()
    weights(0, 1).start()

    @pl.when((me == 0) | (me == last))
    def _():
        pl.semaphore_wait(barrier, 2)

    @pl.when((me > 0) & (me < last))
    def _():
        pl.semaphore_wait(barrier, 3)

    def swapped(source, target, index):
        return pltpu.make_async_remote_copy(
            src_ref=source, dst_ref=target, send_sem=swap_send.at[index], recv_sem=swap_recv.at[index],
            device_id={"col": other}, device_id_type=MESH,
        )

    swap_up = swapped(up_hbm, up_v.at[mine], 0)
    swap_x = swapped(x_hbm, x_v.at[mine], 1)
    swap_up.start()
    swap_x.start()

    span = tokens // pieces
    each = span // tile

    def message(way, kind, u, piece):
        to = lax.rem(me + 1, n_row) if way == 0 else lax.rem(me + n_row - 1, n_row)
        k, slot, at = lax.rem(u, 2), lax.rem(u, ring), slice(piece * span, (piece + 1) * span)
        return pltpu.make_async_remote_copy(
            src_ref=send.at[way, kind, k, at], dst_ref=came.at[way, kind, slot, at],
            send_sem=send_sem.at[way, kind, k, piece], recv_sem=recv_sem.at[way, kind, slot, piece],
            device_id={"row": to}, device_id_type=MESH,
        )

    def relay(way, kind, t):
        place = me if way == 0 else last - me
        u = t - place

        @pl.when((u >= 0) & (u < chunks))
        def _():
            k, slot, at = lax.rem(u, 2), lax.rem(u, ring), lax.rem(u, n_row)
            if kind == 0:
                @pl.when((place < last) & (u >= ring))
                def _():
                    pl.semaphore_wait(credit.at[way], 1)

            for piece in range(pieces):
                @pl.when(place > 0)
                def _():
                    message(way, kind, u, piece).wait_recv()

                @pl.when(place < last)
                def _():
                    @pl.when(u >= 2)
                    def _():
                        message(way, kind, u - 2, piece).wait_send()

                    @pl.when(place > 0)
                    def _():
                        @pl.loop(piece * each, (piece + 1) * each)
                        def _(i):
                            total = wide(part[at, kind, rows(i), :]) + wide(came[way, kind, slot, rows(i), :])
                            send[way, kind, k, rows(i), :] = total.astype(send.dtype)

                    @pl.when(place == 0)
                    def _():
                        @pl.loop(piece * each, (piece + 1) * each)
                        def _(i):
                            send[way, kind, k, rows(i), :] = part[at, kind, rows(i), :]

                    message(way, kind, u, piece).start()

    def step(t, carry):
        now, buf = lax.rem(t, n_row), lax.rem(t, 2)
        f, g = t - last, t - n_row

        @pl.when(t < chunks)
        def _():
            @pl.when(t + 1 < chunks)
            def _():
                for which in range(2):
                    weights(t + 1, which).start()

            weights(t, 0).wait()
            for b in range(width // BLK):
                at = slice(b * BLK, (b + 1) * BLK)
                on = m2_ref[t, b:b + 1, :].astype(w2_m.dtype)
                w2_m[at, :] = w2_buf[buf, at, :] * jnp.broadcast_to(on, (BLK, depth))

            @pl.when(t == 0)
            def _():
                own_up.wait()
                swap_up.wait_recv()

            @pl.loop(0, tiles)
            def _(i):
                part[now, 0, rows(i), :] = contract(up_v[rows(i), :], w2_m[...], 1, 1).astype(part.dtype)

        relay(0, 0, t)
        relay(1, 0, t)

        @pl.when((g >= 0) & (g < chunks))
        def _():
            grads(g)

        @pl.when(t < chunks)
        def _():
            weights(t, 1).wait()
            for b in range(depth // BLK):
                at = slice(b * BLK, (b + 1) * BLK)
                on = m1_ref[t, b:b + 1, :].astype(w1_m.dtype)
                w1_m[now, at, :] = w1_buf[buf, at, :] * jnp.broadcast_to(on, (BLK, width))

            @pl.when(t == 0)
            def _():
                own_x.wait()
                swap_x.wait_recv()

            @pl.loop(0, tiles)
            def _(i):
                part[now, 1, rows(i), :] = contract(x_v[rows(i), :], w1_m[now], 1, 0).astype(part.dtype)

        relay(0, 1, t)
        relay(1, 1, t)

        @pl.when(t == 0)
        def _():
            @pl.loop(0, tiles)
            def _(i):
                acc[rows(i), :] = jnp.zeros((tile, depth), acc.dtype)

            for way, end in ((0, 0), (1, last)):
                @pl.when(me == end)
                def _():
                    @pl.loop(0, ring)
                    def _(slot):
                        @pl.loop(0, tiles)
                        def _(i):
                            for kind in range(2):
                                came[way, kind, slot, rows(i), :] = jnp.zeros((tile, width), came.dtype)

        @pl.when((f >= 0) & (f < chunks))
        def _():
            at, slot = lax.rem(f, n_row), lax.rem(f, ring)

            @pl.loop(0, tiles)
            def _(i):
                def total(kind):
                    return (
                        wide(part[at, kind, rows(i), :])
                        + wide(came[0, kind, slot, rows(i), :])
                        + wide(came[1, kind, slot, rows(i), :])
                    )

                preact, back = total(1), total(0)
                gate = jax.nn.sigmoid(preact)
                hid[rows(i), :] = (preact * gate).astype(hid.dtype)
                grad = (back * gate * (1.0 + preact * (1.0 - gate))).astype(hgr.dtype)
                hgr[rows(i), :] = grad
                acc[rows(i), :] += contract(grad, w1_m[at], 1, 1)

            @pl.when(f + ring < chunks)
            def _():
                @pl.when(me > 0)
                def _():
                    pl.semaphore_signal(credit.at[0], inc=1, device_id={"row": me - 1}, device_id_type=MESH)

                @pl.when(me < last)
                def _():
                    pl.semaphore_signal(credit.at[1], inc=1, device_id={"row": me + 1}, device_id_type=MESH)

        return carry

    def stores(g):
        k = lax.rem(g, 2)
        at = pl.ds(pl.multiple_of(g * width, width), width)
        return (
            pltpu.make_async_copy(g1_buf.at[k], g1_hbm.at[:, at], g_sem.at[0, k]),
            pltpu.make_async_copy(g2_buf.at[k], g2_hbm.at[at], g_sem.at[1, k]),
        )

    def grads(g):
        k = lax.rem(g, 2)

        @pl.when(g >= 2)
        def _():
            for copy in stores(g - 2):
                copy.wait()

        for b in range(depth // BLK):
            at = slice(b * BLK, (b + 1) * BLK)
            if b % 2 == 0:
                pair = min(2, depth // BLK - b)
                value = contract(x_v[:, b * BLK:(b + pair) * BLK], hgr[...], 0, 0)
            on = jnp.broadcast_to(m1_ref[g, b:b + 1, :], (BLK, width)) != 0
            piece = value[(b % 2) * BLK:(b % 2 + 1) * BLK]
            g1_buf[k, at, :] = jnp.where(on, piece, 0.0).astype(g1_buf.dtype)
        across = 512 if depth % 512 == 0 else BLK
        for b in range(width // BLK):
            at = slice(b * BLK, (b + 1) * BLK)
            flipped = hid[:, at].T
            for n in range(depth // across):
                cols = slice(n * across, (n + 1) * across)
                value = contract(flipped, up_v[:, cols], 1, 0)
                on = jnp.broadcast_to(m2_ref[g, b:b + 1, cols], (BLK, across)) != 0
                g2_buf[k, at, cols] = jnp.where(on, value, 0.0).astype(g2_buf.dtype)
        for copy in stores(g):
            copy.start()

    lax.fori_loop(0, chunks + last, step, 0)

    @pl.loop(0, half // tile)
    def _(i):
        swap_out[rows(i), :] = acc[rows(other * (half // tile) + i), :].astype(swap_out.dtype)

    exchange = swapped(swap_out, swap_in, 2)
    exchange.start()
    grads(chunks - 1)
    exchange.wait()

    @pl.loop(0, half // tile)
    def _(i):
        at = rows(core * (half // tile) + i)
        own = wide(acc[at, :].astype(swap_out.dtype))
        swap_out[rows(i), :] = (wide(up_v[at, :]) + (own + wide(swap_in[rows(i), :]))).astype(swap_out.dtype)

    result = pltpu.make_async_copy(swap_out, ig_hbm, load_sem.at[0])
    result.start()
    result.wait()
    swap_up.wait_send()
    swap_x.wait_send()
    for g in range(max(0, chunks - 2), chunks):
        for copy in stores(g):
            copy.wait()
    for way in range(2):
        @pl.when((me if way == 0 else last - me) < last)
        def _():
            for kind in range(2):
                for u in range(max(0, chunks - 2), chunks):
                    for piece in range(pieces):
                        message(way, kind, u, piece).wait_send()


def settle_kernel(a_ref, b_ref, a_out, b_out):
    a_out[...] = a_ref[...]
    b_out[...] = b_ref[...]


def settled(first, second):
    depth, hidden = first.shape
    size = 2 * WIDTH if hidden % (2 * WIDTH) == 0 else WIDTH
    across = pl.BlockSpec((depth, size), lambda i: (0, i))
    down = pl.BlockSpec((size, depth), lambda i: (i, 0))
    return pl.pallas_call(
        settle_kernel,
        grid=(hidden // size,),
        out_shape=(
            jax.ShapeDtypeStruct(first.shape, first.dtype),
            jax.ShapeDtypeStruct(second.shape, second.dtype),
        ),
        in_specs=[across, down],
        out_specs=(across, down),
        cost_estimate=pl.CostEstimate(
            flops=0, bytes_accessed=8 * depth * hidden, transcendentals=0
        ),
    )(first, second)


def by_kernel(inputs, upstream, first, on_first, second, on_second):
    n_row = lax.axis_size("row")
    half, depth = upstream.shape
    tokens, hidden = 2 * half, first.shape[1]
    width, chunks, ring = WIDTH, hidden // WIDTH, n_row + 2
    per = width // BLK
    m1 = jnp.repeat(on_first.astype(jnp.float32), BLK, axis=1)
    m1 = m1.reshape(depth // BLK, chunks, width).transpose(1, 0, 2)
    m2 = jnp.repeat(on_second.astype(jnp.float32), BLK, axis=1).reshape(chunks, per, depth)
    bf16 = jnp.bfloat16
    hbm, vmem = pl.BlockSpec(memory_space=pl.ANY), pl.BlockSpec(memory_space=pltpu.VMEM)
    dma = pltpu.SemaphoreType.DMA
    flops = 10 * tokens * depth * hidden
    return pl.pallas_call(
        functools.partial(tick_kernel, n_row, ring, PIECES),
        out_shape=(
            jax.ShapeDtypeStruct((half, depth), bf16),
            jax.ShapeDtypeStruct(first.shape, bf16),
            jax.ShapeDtypeStruct(second.shape, bf16),
        ),
        in_specs=[hbm] * 4 + [vmem] * 2,
        out_specs=(hbm,) * 3,
        scratch_shapes=[
            pltpu.VMEM((tokens, depth), bf16),
            pltpu.VMEM((tokens, depth), bf16),
            pltpu.VMEM((tokens, depth), jnp.float32),
            pltpu.VMEM((2, depth, width), bf16),
            pltpu.VMEM((2, width, depth), bf16),
            pltpu.VMEM((n_row, depth, width), bf16),
            pltpu.VMEM((width, depth), bf16),
            pltpu.VMEM((n_row, 2, tokens, width), bf16),
            pltpu.VMEM((2, 2, ring, tokens, width), bf16),
            pltpu.VMEM((2, 2, 2, tokens, width), bf16),
            pltpu.VMEM((tokens, width), bf16),
            pltpu.VMEM((tokens, width), bf16),
            pltpu.VMEM((2, depth, width), bf16),
            pltpu.VMEM((2, width, depth), bf16),
            pltpu.VMEM((half, depth), bf16),
            pltpu.VMEM((half, depth), bf16),
            dma((2,)),
            dma((3,)),
            dma((3,)),
            dma((2, 2)),
            dma((2, 2, 2, PIECES)),
            dma((2, 2, ring, PIECES)),
            dma((2, 2)),
            pltpu.SemaphoreType.REGULAR((2,)),
        ],
        compiler_params=pltpu.CompilerParams(
            collective_id=0, has_side_effects=True, vmem_limit_bytes=62 * 1024 * 1024
        ),
        cost_estimate=pl.CostEstimate(
            flops=flops, bytes_accessed=8 * depth * hidden, transcendentals=tokens * hidden
        ),
    )(inputs, upstream, first, second, m1, m2)


def masked(weight, blocks_on):
    height, breadth = weight.shape
    shaped = weight.reshape(height // BLK, BLK, breadth // BLK, BLK)
    on = (blocks_on != 0)[:, None, :, None]
    return jnp.where(on, shaped, jnp.zeros_like(shaped)).reshape(height, breadth)


def pick(place, options):
    chosen = None
    for key, value in options:
        if chosen is None:
            chosen = jnp.where(place == key, value, jnp.zeros_like(value))
        else:
            chosen = jnp.where(place == key, value, chosen)
    return chosen


class Line:
    def __init__(self, count, size, upward):
        me = lax.axis_index("row")
        self.count, self.size, self.upward = count, size, upward
        self.place = me if upward else size - 1 - me
        self.came = []

    def device(self, place):
        return place if self.upward else self.size - 1 - place

    def slot(self, partials):
        t = len(self.came)
        senders = [k for k in range(self.size - 1) if 0 <= t - k < self.count]
        send = pick(self.place, [(k, partials[t - k]) for k in senders])
        if t:
            send = (send.astype(jnp.float32) + self.came[-1].astype(jnp.float32)).astype(
                send.dtype
            )
        route = [(self.device(k), self.device(k + 1)) for k in senders]
        self.came.append(lax.ppermute(send, "row", route))

    def before(self, chunk):
        return pick(self.place, [(k, self.came[chunk + k - 1]) for k in range(1, self.size)])


def on_device(stash, slot, cotangent, w_first, mask_first, w_second, mask_second):
    n_row, n_col = lax.axis_size("row"), lax.axis_size("col")
    upstream = cotangent[0]
    inputs = lax.dynamic_index_in_dim(stash[0], slot[0], 0, keepdims=False)
    first, second = w_first[0], w_second[0]
    on_first, on_second = mask_first[0], mask_second[0]
    swap = [(0, 1), (1, 0)]
    n_section = lax.axis_size("section")
    route = [((i + 1) % n_section, i) for i in range(n_section)]
    if n_col == 2 and n_row > 1 and first.shape[1] % WIDTH == 0 and first.shape[1] // WIDTH > n_row + 2:
        input_grad, grad_first, grad_second = by_kernel(
            inputs, upstream, first, on_first, second, on_second
        )
        moved = lax.ppermute(input_grad, "section", route)
        grad_first, grad_second = settled(grad_first, grad_second)
        return moved[None], grad_first[None], grad_second[None]
    if n_col == 2:
        tokens_up = jnp.concatenate([upstream, lax.ppermute(upstream, "col", swap)], axis=0)
        tokens_in = jnp.concatenate([inputs, lax.ppermute(inputs, "col", swap)], axis=0)
    else:
        tokens_up = lax.all_gather(upstream, "col", axis=0, tiled=True)
        tokens_in = lax.all_gather(inputs, "col", axis=0, tiled=True)

    blocks = on_first.shape[1]
    count = max(n for n in range(1, min(blocks, MOST_CHUNKS) + 1) if blocks % n == 0)
    per = blocks // count
    width = per * BLK
    height = first.shape[0]

    sparse_first, pre_parts, back_parts = [], [], []
    lines = {(name, up): Line(count, n_row, up) for name in ("back", "pre") for up in (True, False)}
    grad_first = jnp.zeros(first.shape, jnp.bfloat16)
    grad_second = jnp.zeros(second.shape, jnp.bfloat16)
    total_input = None
    for t in range(count + n_row - 1):
        if t < count:
            cols, blks = slice(t * width, (t + 1) * width), slice(t * per, (t + 1) * per)
            second_c = masked(second[cols], on_second[blks])
            back_parts.append(contract(tokens_up, second_c, 1, 1).astype(jnp.bfloat16))
            first_c = masked(first[:, cols], on_first[:, blks])
            sparse_first.append(first_c)
            pre_parts.append(contract(tokens_in, first_c, 1, 0).astype(jnp.bfloat16))
        if t < count + n_row - 2:
            for name, parts in (("back", back_parts), ("pre", pre_parts)):
                for up in (True, False):
                    lines[name, up].slot(parts)
        c = t - (n_row - 1)
        if c < 0:
            continue

        def total(name, parts):
            whole = parts[c].astype(jnp.float32)
            if n_row > 1:
                for up in (True, False):
                    whole = whole + lines[name, up].before(c).astype(jnp.float32)
            return whole

        preact, back = total("pre", pre_parts), total("back", back_parts)
        gate = jax.nn.sigmoid(preact)
        hidden = (preact * gate).astype(jnp.bfloat16)
        hidden_grad = (back * gate * (1.0 + preact * (1.0 - gate))).astype(jnp.bfloat16)
        blks = slice(c * per, (c + 1) * per)
        term = contract(hidden_grad, sparse_first[c], 1, 1)
        total_input = term if total_input is None else total_input + term
        part = masked(contract(tokens_in, hidden_grad, 0, 0), on_first[:, blks])
        grad_first = lax.dynamic_update_slice(
            grad_first, part.astype(jnp.bfloat16), (0, c * width)
        )
        part = masked(contract(hidden, tokens_up, 0, 0), on_second[blks])
        grad_second = lax.dynamic_update_slice(
            grad_second, part.astype(jnp.bfloat16), (c * width, 0)
        )

    rounded = total_input.astype(jnp.bfloat16)
    if n_col == 2:
        half = upstream.shape[0]
        other = lax.ppermute(rounded[half:], "col", swap)
        summed = rounded[:half].astype(jnp.float32) + other.astype(jnp.float32)
    else:
        summed = lax.psum_scatter(rounded, "col", scatter_dimension=0, tiled=True).astype(
            jnp.float32
        )
    input_grad = (upstream.astype(jnp.float32) + summed).astype(jnp.bfloat16)
    n_section = lax.axis_size("section")
    moved = lax.ppermute(
        input_grad, "section", [((i + 1) % n_section, i) for i in range(n_section)]
    )
    return moved[None], grad_first[None], grad_second[None]


def solution(mesh):
    return jax.shard_map(
        on_device,
        mesh=mesh,
        in_specs=(
            P("section", None, "col", "row"),
            P("section"),
            P("section", "col", "row"),
            P("section", "row", "col"),
            P("section", "row", "col"),
            P("section", "col", "row"),
            P("section", "col", "row"),
        ),
        out_specs=(
            P("section", "col", "row"),
            P("section", "row", "col"),
            P("section", "col", "row"),
        ),
        check_vma=False,
    )
```
